512 devices in a mesh: dp: 32 (over z, y_lo, core), tensor: 16 (over y_hi, x).
Axes of the slice: x: 4, y: 8 (y_hi: 4, y_lo: 2; y = y_hi * 2 + y_lo), z: 8, core: 2. Of those that a mesh axis runs over, the one named last changes fastest.
Arguments:
- tokens: bfloat16 [3072, 8192], P('tensor', 'dp'), may hold values from -6 to 6
- w_gate: bfloat16 [8192, 26624], P('dp', 'tensor'), may hold values from -0.0625 to 0.0625
- gate_pre: bfloat16 [3072, 26624], P('dp', 'tensor'), may hold values from -8 to 8
- up_act: bfloat16 [3072, 26624], P('dp', 'tensor'), may hold values from -6 to 6
- d_hidden: bfloat16 [3072, 26624], P('dp', 'tensor'), may hold values from -6 to 6
- block_mask: int32 [64, 208, 8], P('dp', 'tensor'), may hold values 0 or 1
- lang_ids: int32 [3072], P('tensor'), may hold values from 0 to 7
Outputs:
- input_grad: bfloat16 [3072, 8192], P('tensor', 'dp')
- weight_grad: float32 [8192, 26624], P('dp', 'tensor')
The draws below stay inside these ranges and needn't reach their ends.
All inputs are finite; a program needn't handle non-finite values. No bound on the sum of `block_mask` on one device may be relied on, other than what follows from the above.
Results may differ from the reference program's by a relative error of at most 0.0049.
Values may be sent and summed in bfloat16 or wider, within the bound.
A program may use at most 128 MiB of HBM per device.

```python
import math
import jax
import jax.numpy as jnp
import numpy as np
from jax import lax

D = 8192
FFP = 26624
BLOCK = 128
LANGS = 8
TOKENS = 3072


def touch_ends(drawn, own_key, least, top_value):
    dims = drawn.shape
    spot = [jax.random.randint(jax.random.fold_in(own_key, axis), (), 0, dims[axis]) for axis in range(len(dims))]
    drawn = drawn.at[tuple(spot)].set(least)
    longest = dims.index(max(dims))
    spot[longest] = (spot[longest] + 1) % dims[longest]
    return drawn.at[tuple(spot)].set(top_value)


def spiked(values, own_key, source, target, parts, factor):
    owner, partner = [(jnp.arange(values.shape[position]) // (values.shape[position] // parts)).reshape([-1 if axis == position else 1 for axis in range(values.ndim)]) for position in (source, target)]
    chosen = jax.random.permutation(own_key, parts)[partner]
    strong = (owner == chosen) | (owner == (partner + parts // 2) % parts)
    return jnp.where(strong, factor * values, values)


def level_of(rng, extent, split, low, top_value):
    loudness, own = 1.0, jax.random.fold_in(rng, 6)
    for axis_at, blocks in split:
        steps = jnp.exp(jax.random.uniform(jax.random.fold_in(own, axis_at), (blocks,), jnp.float32, low / len(split), top_value / len(split)))
        loudness = loudness * jnp.repeat(steps, extent[axis_at] // blocks).reshape([-1 if axis == axis_at else 1 for axis in range(len(extent))])
    return loudness


def rank_table(count, skew):
    weights = [(1 << 20) // math.isqrt(rank ** skew) + 1 for rank in range(1, count + 1)]
    deviation = 1 + sum(weights) // (1 << 30)
    return np.cumsum(np.array([max(1, weight // deviation) for weight in weights]))


def ranked(rng, shape, count, slope):
    listing = rank_table(count, slope)
    pick = jax.random.randint(jax.random.fold_in(rng, 1), shape, 0, int(listing[count - 1]))
    grade = jnp.searchsorted(jnp.asarray(listing, jnp.int32), pick, side="right")
    return jax.random.permutation(jax.random.fold_in(rng, 2), count)[grade].astype(jnp.int32)


def bell_draw(rng, dims, deviation, most, shards=(), kind=jnp.bfloat16):
    drawn = deviation * jax.random.normal(rng, dims, jnp.float32)
    if shards:
        drawn = drawn * level_of(rng, dims, shards, -0.22, 0.18)
    return jnp.clip(drawn, -most, most).astype(kind)


def heavy_noise(own_key, dims, width, reach, split, heavy, kind=jnp.bfloat16):
    drawn = width * jax.random.normal(own_key, dims, jnp.float32)
    if split:
        drawn = drawn * level_of(own_key, dims, split, -0.22, 0.18)
    return jnp.clip(spiked(drawn, jax.random.fold_in(own_key, 3), *heavy), -reach, reach).astype(kind)


def setup_inputs(seed: int = 0) -> dict:
    key_of = jax.random.split(jax.random.key(seed), 8)
    return {
        "tokens": bell_draw(key_of[0], (TOKENS, D), 1.0, 6.0, ((0, 16), (1, 32))),
        "w_gate": bell_draw(key_of[1], (D, FFP), D ** -0.5, 0.0625, ((0, 32), (1, 16))),
        "gate_pre": bell_draw(key_of[2], (TOKENS, FFP), 2.0, 8.0, ((0, 32), (1, 16))),
        "up_act": bell_draw(key_of[3], (TOKENS, FFP), 1.0, 6.0, ((0, 32), (1, 16))),
        "d_hidden": heavy_noise(key_of[4], (TOKENS, FFP), 1.0, 6.0, ((0, 32), (1, 16)), (1, 0, 32, 2.75)),
        "block_mask": touch_ends((jax.random.randint(key_of[5], (D // BLOCK, FFP // BLOCK, LANGS), 0, 2) < 1).astype(jnp.int32), jax.random.fold_in(key_of[5], 1), 0, 1),
        "lang_ids": touch_ends(ranked(key_of[6], (TOKENS,), LANGS, 2), jax.random.fold_in(key_of[6], 3), 0, LANGS - 1).astype(jnp.int32),
    }


def reference(tokens, w_gate, gate_pre, up_act, d_hidden, block_mask, lang_ids):
    gate_value = gate_pre.astype(jnp.float32)
    sigmoid_gate = jax.nn.sigmoid(gate_value)
    gate_grad = (d_hidden.astype(jnp.float32) * up_act.astype(jnp.float32) * sigmoid_gate * (1.0 + gate_value * (1.0 - sigmoid_gate))).astype(jnp.bfloat16)
    rows_total = tokens.shape[0]
    onehot = (lang_ids[:, None] == jnp.arange(LANGS, dtype=jnp.int32)[None, :]).astype(jnp.float32)
    mask_table = block_mask.astype(jnp.float32)

    def one_block(block_index):
        table_row = lax.dynamic_index_in_dim(mask_table, block_index, 0, keepdims=False)
        picked = jnp.dot(onehot, table_row.T, preferred_element_type=jnp.float32)
        scaled = (gate_grad.astype(jnp.float32).reshape(rows_total, FFP // BLOCK, BLOCK) * picked[:, :, None]).astype(jnp.bfloat16).reshape(rows_total, FFP)
        w_rows = lax.dynamic_slice_in_dim(w_gate, block_index * BLOCK, BLOCK, 0)
        token_cols = lax.dynamic_slice_in_dim(tokens, block_index * BLOCK, BLOCK, 1)
        input_part = jnp.dot(scaled, w_rows.T, preferred_element_type=jnp.float32)
        weight_part = jnp.dot(token_cols.T, scaled, preferred_element_type=jnp.float32)
        return (input_part, weight_part)
    input_parts, weight_parts = lax.map(one_block, jnp.arange(D // BLOCK, dtype=jnp.int32))
    input_grad = jnp.transpose(input_parts, (1, 0, 2)).reshape(rows_total, D).astype(jnp.bfloat16)
    weight_grad = weight_parts.reshape(D, FFP) / jnp.sqrt(jnp.float32(rows_total))
    return (input_grad, weight_grad)
```

```python
import functools
import math

import jax
import jax.numpy as jnp
from jax import lax
from jax.experimental import pallas as pl
from jax.experimental.pallas import tpu as pltpu
from jax.sharding import PartitionSpec as P

BF = jnp.bfloat16
F32 = jnp.float32
NZ = 8
NX = 4
NH = 4
STAGE_LAG = 3
CONTRACT_ROWS = (((0,), (0,)), ((), ()))
CONTRACT_COLS = (((1,), (1,)), ((), ()))

ROUTES = {
    0: [("up", "all", 1), ("down", "all", 2), ("y", "all", 8)],
    1: [("up", "all", 3), ("y", "all", 9)],
    2: [("down", "all", 4), ("y", "all", 10)],
    3: [("up", "all", 5)],
    4: [("down", "all", 6)],
    5: [("up", "low", 7)],
    6: [("down", "high", 16)],
    7: [],
    8: [],
    9: [("up", "all", 11)],
    10: [("down", "all", 12)],
    11: [("up", "all", 13)],
    12: [("down", "all", 14)],
    13: [("up", "low", 15)],
    14: [("down", "high", 17)],
    15: [],
}
SEND_IDS = {}
for _piece, _sends in ROUTES.items():
    for _n in range(len(_sends)):
        SEND_IDS[(_piece, _n)] = len(SEND_IDS)
N_SENDS = len(SEND_IDS)

EARLY = (8, 3, 4)
AT_STEP = {0: (9, 10), 1: (5, 6), 4: (11, 12), 6: (7,), 9: (13, 14), 13: (15,)}


def kernel(
    rows,
    col_chunks,
    scale,
    packed_ref,
    w_ref,
    gate_ref,
    up_ref,
    dh_ref,
    table_ref,
    out_ref,
    wout_ref,
    grads,
    toks,
    own,
    s1,
    r1,
    s2,
    r2,
    g_send,
    g_recv,
    c_send,
    c_recv,
    t_send,
    t_recv,
    s1_sem,
    r1_sem,
    s2_sem,
    r2_sem,
):
    half = rows // 2
    dp = lax.axis_index("dp")
    tensor = lax.axis_index("tensor")
    core = dp % 2
    y = (dp // 2) % 2
    z = dp // 4
    x = tensor % NX
    yh = tensor // NX

    def dp_of(zz, yy, cc):
        return (zz * 2 + yy) * 2 + cc

    targets = {
        "up": dp_of((z + 1) % NZ, y, core),
        "down": dp_of((z + NZ - 1) % NZ, y, core),
        "y": dp_of(z, 1 - y, core),
        "core": dp_of(z, y, 1 - core),
    }

    def x_peer(step):
        return yh * NX + (x + step) % NX

    def h_peer(step):
        return ((yh + step) % NH) * NX + x

    barrier = pltpu.get_barrier_semaphore()
    for way in ("up", "down", "y", "core"):
        pl.semaphore_signal(
            barrier, inc=1, device_id={"dp": targets[way]}, device_id_type=pl.DeviceIdType.MESH
        )
    for step in range(1, 4):
        for peer in (x_peer(step), h_peer(step)):
            pl.semaphore_signal(
                barrier, inc=1, device_id={"tensor": peer}, device_id_type=pl.DeviceIdType.MESH
            )

    def slot_of(piece):
        r = piece % 8
        dz = ((r + 1) // 2) * (2 * ((r + 1) % 2) - 1)
        return 2 * ((z + dz + NZ) % NZ) + (y + piece // 8) % 2

    def span(part, cc):
        start = cc * half
        if part == "high":
            start = start + half // 2
        return pl.ds(pl.multiple_of(start, 16), half if part == "all" else half // 2)

    def gate_copy(piece, part, way, ssem, rsem):
        view = grads.at[slot_of(piece), span(part, core), :]
        return pltpu.make_async_remote_copy(
            src_ref=view,
            dst_ref=view,
            send_sem=ssem,
            recv_sem=rsem,
            device_id={"dp": targets[way]},
            device_id_type=pl.DeviceIdType.MESH,
        )

    def route_copy(piece, n):
        way, part, rsem = ROUTES[piece][n]
        return gate_copy(piece, part, way, g_send.at[SEND_IDS[(piece, n)]], g_recv.at[rsem])

    def core_copy(piece):
        return gate_copy(piece, "all", "core", c_send.at[piece], c_recv.at[piece])

    def arrived(piece):
        if piece in (7, 15):
            gate_copy(piece, "low", "y", g_send.at[0], g_recv.at[piece]).wait_recv()
            gate_copy(piece, "high", "y", g_send.at[0], g_recv.at[16 + piece // 8]).wait_recv()
        else:
            gate_copy(piece, "all", "y", g_send.at[0], g_recv.at[piece]).wait_recv()

    def pass_on(piece):
        for n in range(len(ROUTES[piece])):
            route_copy(piece, n).start()
        core_copy(piece).start()

    def handle(piece):
        arrived(piece)
        pass_on(piece)

    def tok_copy(src, block, peer, ssem):
        return pltpu.make_async_remote_copy(
            src_ref=src,
            dst_ref=toks.at[block],
            send_sem=ssem,
            recv_sem=t_recv.at[block],
            device_id={"tensor": peer},
            device_id_type=pl.DeviceIdType.MESH,
        )

    def tok_own(n):
        peer = h_peer(n + 1) if n < 3 else x_peer(n - 2)
        return tok_copy(packed_ref, tensor, peer, t_send.at[n])

    def tok_fwd(hstep, xstep):
        block = h_peer(hstep)
        return tok_copy(
            toks.at[block], block, x_peer(xstep), t_send.at[6 + (hstep - 1) * 3 + xstep - 1]
        )

    def tok_arrived(block):
        tok_copy(packed_ref, block, tensor, t_send.at[0]).wait_recv()

    mine = slot_of(0)
    for lo, hi in col_chunks:
        g = gate_ref[:, lo:hi].astype(F32)
        s = jax.nn.sigmoid(g)
        grads[mine, span("all", core), lo:hi] = (
            dh_ref[:, lo:hi].astype(F32) * up_ref[:, lo:hi].astype(F32) * s * (1.0 + g * (1.0 - s))
        ).astype(BF)
    toks[tensor] = packed_ref[...]
    wout_ref[...] = jnp.zeros_like(wout_ref)
    pl.semaphore_wait(barrier, 10)

    pass_on(0)
    for n in range(6):
        tok_own(n).start()
    for hstep in (1, 3):
        tok_arrived(h_peer(hstep))
        for xstep in range(1, 4):
            tok_fwd(hstep, xstep).start()
    for piece in (1, 2):
        handle(piece)
    tok_arrived(h_peer(2))
    for xstep in range(1, 4):
        tok_fwd(2, xstep).start()
    for piece in EARLY:
        handle(piece)
    for xstep in range(1, 4):
        for hstep in range(4):
            tok_arrived(((yh + hstep) % NH) * NX + (x + xstep) % NX)

    def sum_copy(piece, slot):
        return pltpu.make_async_remote_copy(
            src_ref=s1.at[piece],
            dst_ref=r1.at[x * NH + slot // NX],
            send_sem=s1_sem.at[piece],
            recv_sem=r1_sem.at[x * NH + slot // NX],
            device_id={"tensor": yh * NX + slot % NX},
            device_id_type=pl.DeviceIdType.MESH,
        )

    def sum_arrived(index):
        pltpu.make_async_remote_copy(
            src_ref=s1.at[0],
            dst_ref=r1.at[index],
            send_sem=s1_sem.at[0],
            recv_sem=r1_sem.at[index],
            device_id={"tensor": tensor},
            device_id_type=pl.DeviceIdType.MESH,
        ).wait_recv()

    def total_copy(to_h):
        return pltpu.make_async_remote_copy(
            src_ref=s2.at[to_h],
            dst_ref=r2.at[yh],
            send_sem=s2_sem.at[to_h],
            recv_sem=r2_sem.at[yh],
            device_id={"tensor": to_h * NX + x},
            device_id_type=pl.DeviceIdType.MESH,
        )

    def step_body(step, carry):
        for at, pieces in AT_STEP.items():

            @pl.when(step == at)
            def _():
                for piece in pieces:
                    handle(piece)

        @pl.when(step < 16)
        def _():
            slot = slot_of(step)
            other = grads.at[slot, span("all", 1 - core), :]
            pltpu.make_async_remote_copy(
                src_ref=other,
                dst_ref=other,
                send_sem=c_send.at[0],
                recv_sem=c_recv.at[step],
                device_id={"dp": targets["core"]},
                device_id_type=pl.DeviceIdType.MESH,
            ).wait_recv()
            onehot = toks[slot, rows:, :rows]
            parts = []
            for a in range(2):
                data = toks[slot, :rows, a * 128 : (a + 1) * 128]
                part = None
                for lo, hi in col_chunks:
                    mask = lax.dot_general(
                        onehot, table_ref[a, :, lo:hi], CONTRACT_ROWS, preferred_element_type=F32
                    )
                    scaled = grads[slot, :, lo:hi] * mask.astype(BF)
                    term = lax.dot_general(
                        scaled,
                        w_ref[a * 128 : (a + 1) * 128, lo:hi],
                        CONTRACT_COLS,
                        preferred_element_type=F32,
                    )
                    part = term if part is None else part + term
                    wout_ref[a * 128 : (a + 1) * 128, lo:hi] += lax.dot_general(
                        data, scaled, CONTRACT_ROWS, preferred_element_type=F32
                    )
                parts.append(part)
            part = jnp.concatenate(parts, axis=1)

            @pl.when(slot % NX == x)
            def _():
                own[slot // NX] = part

            @pl.when(slot % NX != x)
            def _():
                s1[step] = part.astype(BF)
                sum_copy(step, slot).start()

        @pl.when(step >= STAGE_LAG)
        def _():
            slot = slot_of(step - STAGE_LAG)
            to_h = slot // NX

            @pl.when(slot % NX == x)
            def _():
                total = own[to_h]
                for xstep in range(1, 4):
                    index = ((x + xstep) % NX) * NH + to_h
                    sum_arrived(index)
                    total = total + r1[index].astype(F32)

                @pl.when(to_h == yh)
                def _():
                    own[to_h] = total

                @pl.when(to_h != yh)
                def _():
                    s2[to_h] = total.astype(BF)
                    total_copy(to_h).start()

        return carry

    lax.fori_loop(0, 16 + STAGE_LAG, step_body, 0)

    wout_ref[...] = wout_ref[...] * scale

    total = own[yh]
    for hstep in range(1, 4):
        src = (yh + hstep) % NH
        pltpu.make_async_remote_copy(
            src_ref=s2.at[0],
            dst_ref=r2.at[src],
            send_sem=s2_sem.at[0],
            recv_sem=r2_sem.at[src],
            device_id={"tensor": tensor},
            device_id_type=pl.DeviceIdType.MESH,
        ).wait_recv()
        total = total + r2[src].astype(F32)
    out_ref[...] = total.astype(BF)

    for piece in range(16):
        for n in range(len(ROUTES[piece])):
            route_copy(piece, n).wait_send()
        core_copy(piece).wait_send()
    for n in range(6):
        tok_own(n).wait_send()
    for hstep in range(1, 4):
        for xstep in range(1, 4):
            tok_fwd(hstep, xstep).wait_send()
        total_copy((yh + hstep) % NH).wait_send()

    def drain(step, carry):
        slot = slot_of(step)

        @pl.when(slot % NX != x)
        def _():
            sum_copy(step, slot).wait_send()

        return carry

    lax.fori_loop(0, 16, drain, 0)


def local(tokens, w_gate, gate_pre, up_act, d_hidden, block_mask, lang_ids):
    rows, width = tokens.shape
    hidden = w_gate.shape[1]
    row_blocks, col_blocks, langs = block_mask.shape
    table = jnp.broadcast_to(
        jnp.transpose(block_mask.astype(BF), (0, 2, 1))[:, :, :, None],
        (row_blocks, langs, col_blocks, hidden // col_blocks),
    ).reshape(row_blocks, langs, hidden)
    table = jnp.pad(table, ((0, 0), (0, 16 - langs), (0, 0)))
    onehot = (lang_ids[None, :] == jnp.arange(16, dtype=jnp.int32)[:, None]).astype(BF)
    packed = jnp.concatenate([tokens, jnp.pad(onehot, ((0, 0), (0, width - rows)))], axis=0)
    col_chunks = ((0, 512), (512, 1024), (1024, hidden))
    dma = pltpu.SemaphoreType.DMA
    vmem = pl.BlockSpec(memory_space=pltpu.VMEM)
    return tuple(
        pl.pallas_call(
            functools.partial(kernel, rows, col_chunks, 1.0 / math.sqrt(16 * rows)),
            out_shape=(
                jax.ShapeDtypeStruct((rows, width), BF),
                jax.ShapeDtypeStruct((width, hidden), F32),
            ),
            in_specs=[vmem] * 6,
            out_specs=(vmem, vmem),
            scratch_shapes=[
                pltpu.VMEM((16, rows, hidden), BF),
                pltpu.VMEM((16, rows + 16, width), BF),
                pltpu.VMEM((NH, rows, width), F32),
                pltpu.VMEM((16, rows, width), BF),
                pltpu.VMEM((16, rows, width), BF),
                pltpu.VMEM((NH, rows, width), BF),
                pltpu.VMEM((NH, rows, width), BF),
                dma((N_SENDS,)),
                dma((18,)),
                dma((16,)),
                dma((16,)),
                dma((15,)),
                dma((16,)),
                dma((16,)),
                dma((16,)),
                dma((NH,)),
                dma((NH,)),
            ],
            compiler_params=pltpu.CompilerParams(collective_id=0, has_side_effects=True),
        )(packed, w_gate, gate_pre, up_act, d_hidden, table)
    )


def solution(mesh):
    placed = (
        P("tensor", "dp"),
        P("dp", "tensor"),
        P("dp", "tensor"),
        P("dp", "tensor"),
        P("dp", "tensor"),
        P("dp", "tensor", None),
        P("tensor"),
    )
    return jax.shard_map(
        local,
        mesh=mesh,
        in_specs=placed,
        out_specs=(P("tensor", "dp"), P("dp", "tensor")),
        check_vma=False,
    )
```

```python
import functools
import math

import jax
import jax.numpy as jnp
from jax import lax
from jax.experimental import pallas as pl
from jax.experimental.pallas import tpu as pltpu
from jax.sharding import PartitionSpec as P

BF = jnp.bfloat16
F32 = jnp.float32
NZ = 8
NX = 4
NH = 4
STAGE_LAG = 3
CONTRACT_ROWS = (((0,), (0,)), ((), ()))
CONTRACT_COLS = (((1,), (1,)), ((), ()))

ROUTES = {(piece, h): [] for piece in range(16) for h in range(2)}
for _h in range(2):
    ROUTES[0, _h] = [("up", 1), ("down", 2), ("y", 8)]
    ROUTES[1, _h] = [("up", 3), ("y", 9)]
    ROUTES[2, _h] = [("down", 4), ("y", 10)]
    for _p in (3, 9, 11):
        ROUTES[_p, _h] = [("up", _p + 2)]
    for _p in (4, 10, 12):
        ROUTES[_p, _h] = [("down", _p + 2)]
ROUTES[5, 0] = [("up", 7)]
ROUTES[6, 1] = [("down", 7)]
ROUTES[13, 0] = [("up", 15)]
ROUTES[14, 1] = [("down", 15)]
SENDS = [(piece, h, way, to) for (piece, h), way_to in ROUTES.items() for way, to in way_to]
SEND_ID = {(piece, h, way): n for n, (piece, h, way, _) in enumerate(SENDS)}
N_SENDS = len(SENDS)


AT_STEP = {
    1: ((5, 0), (6, 0)),
    3: ((5, 1), (6, 1), (9, 0), (10, 0)),
    4: ((9, 1), (10, 1)),
    6: ((7, 0), (7, 1)),
    7: ((8, 0), (8, 1)),
    9: ((11, 0), (12, 0)),
    10: ((11, 1), (12, 1)),
    12: ((13, 0), (14, 0)),
    13: ((13, 1), (14, 1)),
    15: ((15, 0), (15, 1)),
}


def kernel(
    rows,
    col_chunks,
    tok_ref,
    ids_ref,
    bits_ref,
    w_ref,
    gate_ref,
    up_ref,
    dh_ref,
    out_ref,
    wout_ref,
    table_ref,
    grads,
    toks,
    own,
    s1,
    r1,
    s2,
    r2,
    g_send,
    g_recv,
    c_send,
    c_recv,
    t_send,
    t_recv,
    s1_sem,
    r1_sem,
    s2_sem,
    r2_sem,
):
    half = rows // 2
    dp = lax.axis_index("dp")
    tensor = lax.axis_index("tensor")
    core = dp % 2
    y = (dp // 2) % 2
    z = dp // 4
    x = tensor % NX
    yh = tensor // NX

    def dp_of(zz, yy, cc):
        return (zz * 2 + yy) * 2 + cc

    targets = {
        "up": dp_of((z + 1) % NZ, y, core),
        "down": dp_of((z + NZ - 1) % NZ, y, core),
        "y": dp_of(z, 1 - y, core),
        "core": dp_of(z, y, 1 - core),
    }

    def x_peer(step):
        return yh * NX + (x + step) % NX

    def h_peer(step):
        return ((yh + step) % NH) * NX + x

    barrier = pltpu.get_barrier_semaphore()
    for way in ("up", "down", "y", "core"):
        pl.semaphore_signal(
            barrier, inc=1, device_id={"dp": targets[way]}, device_id_type=pl.DeviceIdType.MESH
        )
    for step in range(1, 4):
        for peer in (x_peer(step), h_peer(step)):
            pl.semaphore_signal(
                barrier, inc=1, device_id={"tensor": peer}, device_id_type=pl.DeviceIdType.MESH
            )

    def slot_of(piece):
        r = piece % 8
        dz = ((r + 1) // 2) * (2 * ((r + 1) % 2) - 1)
        return 2 * ((z + dz + NZ) % NZ) + (y + piece // 8) % 2

    def span(h, cc):
        start = cc * half if h is None else cc * half + h * (half // 2)
        return pl.ds(pl.multiple_of(start, 16), half if h is None else half // 2)

    def gate_copy(piece, h, way, ssem, rsem):
        view = grads.at[slot_of(piece), span(h, core), :]
        return pltpu.make_async_remote_copy(
            src_ref=view,
            dst_ref=view,
            send_sem=ssem,
            recv_sem=rsem,
            device_id={"dp": targets[way]},
            device_id_type=pl.DeviceIdType.MESH,
        )

    def route_copy(piece, h, way, to):
        return gate_copy(piece, h, way, g_send.at[SEND_ID[piece, h, way]], g_recv.at[2 * to + h])

    def core_copy(piece):
        return gate_copy(piece, None, "core", c_send.at[piece], c_recv.at[piece])

    def pass_on(piece, h, ways=("up", "down", "y")):
        for way, to in ROUTES[piece, h]:
            if way in ways:
                route_copy(piece, h, way, to).start()

    def handle(piece, h):
        gate_copy(piece, h, "y", g_send.at[0], g_recv.at[2 * piece + h]).wait_recv()
        pass_on(piece, h)
        if h == 1:
            core_copy(piece).start()

    def tok_copy(block, part, peer, ssem):
        view = toks.at[block]
        if part is not None:
            view = toks.at[block, pl.ds(112 * part, 112 - 16 * part), :]
        return pltpu.make_async_remote_copy(
            src_ref=view,
            dst_ref=view,
            send_sem=ssem,
            recv_sem=t_recv.at[block + 16 * (part or 0)],
            device_id={"tensor": peer},
            device_id_type=pl.DeviceIdType.MESH,
        )

    def block_at(hstep, xstep):
        return ((yh + hstep) % NH) * NX + (x + xstep) % NX

    tok_sends = []
    for side in (1, 3):
        tok_sends.append((0, 0, None, side, 0))
        tok_sends.append((0, 0, None, 0, side))
    for hstep in range(4):
        for side, part in ((3, 0), (1, 1)):
            tok_sends.append((hstep, side, part, 0, 4 - side))
    for hstep in (1, 2, 3):
        for side in (1, 3):
            tok_sends.append((hstep, 0, None, 0, side))
    for side, part in ((3, 0), (1, 1)):
        tok_sends.append((side, 0, part, 4 - side, 0))

    def tok_send(send):
        hstep, xstep, part, to_h, to_x = send
        return tok_copy(
            block_at(hstep, xstep), part, block_at(to_h, to_x), t_send.at[tok_sends.index(send)]
        )

    def tok_arrived(hstep, xstep):
        block = block_at(hstep, xstep)
        if hstep == 2 and xstep == 0 or xstep == 2:
            tok_copy(block, 0, tensor, t_send.at[0]).wait_recv()
            tok_copy(block, 1, tensor, t_send.at[0]).wait_recv()
        else:
            tok_copy(block, None, tensor, t_send.at[0]).wait_recv()

    def tok_handle(hstep, xstep):
        if (hstep, xstep) != (0, 0):
            tok_arrived(hstep, xstep)
        for send in tok_sends:
            if send[:2] == (hstep, xstep):
                tok_send(send).start()

    count = ids_ref.shape[1]
    toks[tensor, :rows, :] = tok_ref[...]
    row = lax.broadcasted_iota(jnp.int32, (16, count), 0)
    same = jnp.where(row == ids_ref[...], 1.0, 0.0).astype(BF)
    toks[tensor, rows:, :count] = same
    mine = slot_of(0)
    for lo, hi in col_chunks:
        g = gate_ref[:, lo:hi].astype(F32)
        s = jax.nn.sigmoid(g)
        grads[mine, span(None, core), lo:hi] = (
            dh_ref[:, lo:hi].astype(F32) * up_ref[:, lo:hi].astype(F32) * s * (1.0 + g * (1.0 - s))
        ).astype(BF)
    pl.semaphore_wait(barrier, 10)

    tok_handle(0, 0)
    pass_on(0, 0, ("up", "down"))
    pass_on(0, 1, ("up", "down"))
    core_copy(0).start()

    hidden = wout_ref.shape[1]
    langs, col_blocks = bits_ref.shape[1:]
    lane = lax.broadcasted_iota(jnp.int32, (col_blocks, hidden), 1)
    first = lax.broadcasted_iota(jnp.int32, (col_blocks, hidden), 0) * 128
    spread = jnp.where((lane >= first) & (lane < first + 128), 1.0, 0.0).astype(BF)
    for a in range(2):
        bits = bits_ref[a].astype(F32).astype(BF)
        wide = jnp.dot(bits, spread, preferred_element_type=F32)
        table_ref[a] = jnp.concatenate([wide, jnp.zeros((16 - langs, hidden), F32)], axis=0).astype(BF)
    wout_ref[...] = jnp.zeros_like(wout_ref)

    tok_handle(0, 1)
    tok_handle(0, 3)
    handle(1, 0)
    handle(2, 0)
    tok_handle(1, 0)
    tok_handle(3, 0)
    handle(1, 1)
    handle(2, 1)
    pass_on(0, 0, ("y",))
    pass_on(0, 1, ("y",))
    for side in (1, 3):
        tok_handle(1, side)
        tok_handle(3, side)
    handle(3, 0)
    handle(4, 0)
    tok_handle(2, 0)
    handle(3, 1)
    handle(4, 1)
    tok_handle(2, 1)
    tok_handle(2, 3)

    def sum_copy(piece, slot):
        return pltpu.make_async_remote_copy(
            src_ref=s1.at[piece],
            dst_ref=r1.at[x * NH + slot // NX],
            send_sem=s1_sem.at[piece],
            recv_sem=r1_sem.at[x * NH + slot // NX],
            device_id={"tensor": yh * NX + slot % NX},
            device_id_type=pl.DeviceIdType.MESH,
        )

    def sum_arrived(index):
        pltpu.make_async_remote_copy(
            src_ref=s1.at[0],
            dst_ref=r1.at[index],
            send_sem=s1_sem.at[0],
            recv_sem=r1_sem.at[index],
            device_id={"tensor": tensor},
            device_id_type=pl.DeviceIdType.MESH,
        ).wait_recv()

    def total_copy(to_h):
        return pltpu.make_async_remote_copy(
            src_ref=s2.at[to_h],
            dst_ref=r2.at[yh],
            send_sem=s2_sem.at[to_h],
            recv_sem=r2_sem.at[yh],
            device_id={"tensor": to_h * NX + x},
            device_id_type=pl.DeviceIdType.MESH,
        )

    def step_body(step, carry):
        for at, pieces in AT_STEP.items():

            @pl.when(step == at)
            def _():
                for piece, h in pieces:
                    handle(piece, h)

        @pl.when(step < 16)
        def _():
            slot = slot_of(step)
            other = grads.at[slot, span(None, 1 - core), :]
            pltpu.make_async_remote_copy(
                src_ref=other,
                dst_ref=other,
                send_sem=c_send.at[0],
                recv_sem=c_recv.at[step],
                device_id={"dp": targets["core"]},
                device_id_type=pl.DeviceIdType.MESH,
            ).wait_recv()

            @pl.when((slot + NX - x) % NX == 2)
            def _():
                tok_copy(slot, 0, tensor, t_send.at[0]).wait_recv()
                tok_copy(slot, 1, tensor, t_send.at[0]).wait_recv()

            onehot = toks[slot, rows:, :rows]
            parts = []
            for a in range(2):
                data = toks[slot, :rows, a * 128 : (a + 1) * 128]
                part = None
                for lo, hi in col_chunks:
                    mask = lax.dot_general(
                        onehot, table_ref[a, :, lo:hi], CONTRACT_ROWS, preferred_element_type=F32
                    )
                    scaled = grads[slot, :, lo:hi] * mask.astype(BF)
                    term = lax.dot_general(
                        scaled,
                        w_ref[a * 128 : (a + 1) * 128, lo:hi],
                        CONTRACT_COLS,
                        preferred_element_type=F32,
                    )
                    part = term if part is None else part + term
                    wout_ref[a * 128 : (a + 1) * 128, lo:hi] += lax.dot_general(
                        data, scaled, CONTRACT_ROWS, preferred_element_type=F32
                    )
                parts.append(part)
            part = jnp.concatenate(parts, axis=1)

            @pl.when(slot % NX == x)
            def _():
                own[slot // NX] = part

            @pl.when(slot % NX != x)
            def _():
                s1[step] = part.astype(BF)
                sum_copy(step, slot).start()

        @pl.when(step >= STAGE_LAG)
        def _():
            slot = slot_of(step - STAGE_LAG)
            to_h = slot // NX

            @pl.when(slot % NX == x)
            def _():
                total = own[to_h]
                for xstep in range(1, 4):
                    index = ((x + xstep) % NX) * NH + to_h
                    sum_arrived(index)
                    total = total + r1[index].astype(F32)

                @pl.when(to_h == yh)
                def _():
                    own[to_h] = total

                @pl.when(to_h != yh)
                def _():
                    s2[to_h] = total.astype(BF)
                    total_copy(to_h).start()

        return carry

    lax.fori_loop(0, 16 + STAGE_LAG, step_body, 0)

    total = own[yh]
    for hstep in range(1, 4):
        src = (yh + hstep) % NH
        pltpu.make_async_remote_copy(
            src_ref=s2.at[0],
            dst_ref=r2.at[src],
            send_sem=s2_sem.at[0],
            recv_sem=r2_sem.at[src],
            device_id={"tensor": tensor},
            device_id_type=pl.DeviceIdType.MESH,
        ).wait_recv()
        total = total + r2[src].astype(F32)
    out_ref[...] = total.astype(BF)

    for send in SENDS:
        route_copy(*send).wait_send()
    for piece in range(16):
        core_copy(piece).wait_send()
    for send in tok_sends:
        tok_send(send).wait_send()
    for hstep in range(1, 4):
        total_copy((yh + hstep) % NH).wait_send()

    def drain(step, carry):
        slot = slot_of(step)

        @pl.when(slot % NX != x)
        def _():
            sum_copy(step, slot).wait_send()

        return carry

    lax.fori_loop(0, 16, drain, 0)


def local(tokens, w_gate, gate_pre, up_act, d_hidden, block_mask, lang_ids):
    rows, width = tokens.shape
    hidden = w_gate.shape[1]
    ids = lang_ids.reshape(1, rows)
    bits = jnp.transpose(block_mask, (0, 2, 1))
    col_chunks = ((0, 512), (512, 1024), (1024, hidden))
    dma = pltpu.SemaphoreType.DMA
    vmem = pl.BlockSpec(memory_space=pltpu.VMEM)
    input_grad, weights_sum = pl.pallas_call(
        functools.partial(kernel, rows, col_chunks),
        out_shape=(
            jax.ShapeDtypeStruct((rows, width), BF),
            jax.ShapeDtypeStruct((width, hidden), F32),
        ),
        in_specs=[vmem] * 7,
        out_specs=(vmem, vmem),
        scratch_shapes=[
            pltpu.VMEM((2, 16, hidden), BF),
            pltpu.VMEM((16, rows, hidden), BF),
            pltpu.VMEM((16, rows + 16, width), BF),
            pltpu.VMEM((NH, rows, width), F32),
            pltpu.VMEM((16, rows, width), BF),
            pltpu.VMEM((16, rows, width), BF),
            pltpu.VMEM((NH, rows, width), BF),
            pltpu.VMEM((NH, rows, width), BF),
            dma((N_SENDS,)),
            dma((32,)),
            dma((16,)),
            dma((16,)),
            dma((20,)),
            dma((32,)),
            dma((16,)),
            dma((16,)),
            dma((NH,)),
            dma((NH,)),
        ],
        compiler_params=pltpu.CompilerParams(collective_id=0, has_side_effects=True),
    )(tokens, ids, bits, w_gate, gate_pre, up_act, d_hidden)
    return input_grad, weights_sum * (1.0 / math.sqrt(16 * rows))


def solution(mesh):
    placed = (
        P("tensor", "dp"),
        P("dp", "tensor"),
        P("dp", "tensor"),
        P("dp", "tensor"),
        P("dp", "tensor"),
        P("dp", "tensor", None),
        P("tensor"),
    )
    return jax.shard_map(
        local,
        mesh=mesh,
        in_specs=placed,
        out_specs=(P("tensor", "dp"), P("dp", "tensor")),
        check_vma=False,
    )
```
